128 devices in a mesh: gy: 16 (over y_hi, z, core), gz: 8 (over y_lo, x).
Axes of the slice: x: 4, y: 4 (y_hi: 2, y_lo: 2; y = y_hi * 2 + y_lo), z: 4, core: 2. Of those that a mesh axis runs over, the one named last changes fastest.
Arguments:
- pressure_old: float32 [256, 256, 512], P('gy', 'gz'), may hold values from -4 to 0
- soil_class: int32 [256, 256, 512], P('gy', 'gz'), may hold values from 0 to 11
- top_code: int32 [256, 512], P('gy'), may hold values from 0 to 2
- retention_scale: float32 [12], replicated, may hold values from 0.5 to 4
- retention_power: float32 [12], replicated, may hold values from 2 to 3
- conductivity_sat: float32 [12], replicated, may hold values from 0.2 to 5
- porosity: float32 [12], replicated, may hold values from 0.3 to 0.5
- lift_weight: float32 [2, 32], replicated, may hold values from -4 to 4
- spectral_weight: bfloat16 [32, 32, 32, 1024], P('gy', 'gz'), may hold values from -4 to 4
- local_weight: bfloat16 [32, 32], replicated, may hold values from -1 to 1
- local_bias: float32 [32], replicated, may hold values from -3 to 3
- project_weight: bfloat16 [32, 128], replicated, may hold values from -1 to 1
- project_bias: float32 [128], replicated, may hold values from -3 to 3
- output_weight: bfloat16 [128], replicated, may hold values from -0.5 to 0.5
Outputs:
- pressure_new: float32 [256, 256, 512], P('gy', 'gz')
- residual: float32 [256, 256, 512], P('gy', 'gz')
The draws below stay inside these ranges and needn't reach their ends.
All inputs are finite; a program needn't handle non-finite values.
Results may differ from the reference program's by a relative error of at most 0.014.
The reference program's roundings to bfloat16 on the way count: a program that leaves them out, or rounds other values in their place, can miss the bound.
Values sent between devices are 32-bit elements; how exact they have to be, the bound alone decides.
A program may use at most 128 MiB of HBM per device.

```python
import math
import jax
import jax.numpy as jnp
from jax import lax

NX = 512
M = 16
C = 32
QH = 128
S = 12
F = 2
NY = 256
NZ = 256


def draw_spectral_weight(key, part):
    spans = 2 * M
    rows = jnp.arange(spans, dtype=jnp.int32)
    freq = jnp.where(rows < M, rows + 1, rows - M + 1).astype(jnp.float32)
    lanes = jnp.arange(spans * C, dtype=jnp.int32) // C
    freq_d = freq[lanes]
    freq_a = freq[:, None, None, None]
    freq_b = freq[None, :, None, None]
    freq_last = freq_d[None, None, None, :]
    highest_freq = jnp.maximum(jnp.maximum(freq_a, freq_b), freq_last) / M
    fourth = highest_freq * highest_freq * highest_freq * highest_freq
    factor = 0.15 + 0.85 * fourth
    shape = (spans, spans, C, spans * C)
    key_sign, key_size = jax.random.split(jax.random.fold_in(key, 17))
    signs = jnp.where(jax.random.bernoulli(key_sign, 0.5, shape), 1.0, -1.0).astype(jnp.float32)
    sizes = jax.random.uniform(key_size, shape, jnp.float32, 0.7, 1.0)
    return (4.0 * factor * sizes * signs).astype(jnp.bfloat16)


def plant(values, own_key, low, largest):
    place = [jax.random.randint(jax.random.fold_in(own_key, axis), (), 0, length) for axis, length in enumerate(values.shape)]
    longest = values.shape.index(max(values.shape))
    beside = place[:longest] + [(place[longest] + 1) % values.shape[longest]] + place[longest + 1:]
    return values.at[tuple(place)].set(low).at[tuple(beside)].set(largest)


def levels(rng, shape, cuts, smallest, top_value):
    factor_of = 1.0
    for dim, blocks in cuts:
        heights = jax.random.uniform(jax.random.fold_in(jax.random.fold_in(rng, 6), dim), (blocks,), jnp.float32, smallest / len(cuts), top_value / len(cuts))
        factor_of = factor_of * jnp.repeat(jnp.exp(heights), shape[dim] // blocks).reshape((-1,) + (1,) * (len(shape) - 1 - dim))
    return factor_of


def noise(stream_key, shape, spread, reach, kind=jnp.bfloat16):
    return jnp.clip(spread * jax.random.normal(stream_key, shape, jnp.float32), -reach, reach).astype(kind)


def setup_inputs(seed: int = 0) -> dict:
    key_of = jax.random.split(jax.random.key(seed), 15)
    return {
        "pressure_old": jnp.clip(-4.0 + 4.0 * jax.random.uniform(key_of[0], (NY, NZ, NX), jnp.float32) ** levels(key_of[0], (NY, NZ, NX), ((0, 16), (1, 8)), -0.2, 0.2), -4.0, 0.0),
        "soil_class": plant(jax.random.randint(key_of[1], (NY, NZ, NX), 0, S), jax.random.fold_in(key_of[1], 1), 0, S - 1).astype(jnp.int32),
        "top_code": plant(jax.random.randint(key_of[2], (NY, NX), 0, 3), jax.random.fold_in(key_of[2], 1), 0, 2).astype(jnp.int32),
        "retention_scale": jnp.clip(jnp.exp(jax.random.uniform(key_of[3], (S,), jnp.float32, math.log(0.5), math.log(4.0))), 0.5, 4.0),
        "retention_power": jnp.clip(jax.random.uniform(key_of[4], (S,), jnp.float32, 2.0, 3.0), 2.0, 3.0),
        "conductivity_sat": jnp.clip(jnp.exp(jax.random.uniform(key_of[5], (S,), jnp.float32, math.log(0.2), math.log(5.0))), 0.2, 5.0),
        "porosity": jnp.clip(jax.random.uniform(key_of[6], (S,), jnp.float32, 0.3, 0.5), 0.3, 0.5),
        "lift_weight": noise(key_of[7], (F, C), F ** -0.5, 4.0, jnp.float32),
        "spectral_weight": draw_spectral_weight(jax.random.fold_in(key_of[14], 71), 0),
        "local_weight": noise(key_of[9], (C, C), C ** -0.5, 1.0),
        "local_bias": noise(key_of[10], (C,), 0.5, 3.0, jnp.float32),
        "project_weight": noise(key_of[11], (C, QH), C ** -0.5, 1.0),
        "project_bias": noise(key_of[12], (QH,), 0.5, 3.0, jnp.float32),
        "output_weight": noise(key_of[13], (QH,), QH ** -0.5, 0.5),
    }


RAINFALL = 0.5
STORAGE = 20.0

def fourier_table(length, first, count, modes):
    rows = jnp.arange(2 * modes, dtype=jnp.int32)
    freq = jnp.where(rows < modes, rows + 1, rows - modes + 1)
    cells = first + jnp.arange(count, dtype=jnp.int32)
    phase = jnp.mod(freq[:, None] * cells[None, :], length).astype(jnp.float32) * (2.0 * math.pi / length)
    return jnp.where((rows < modes)[:, None], jnp.cos(phase), jnp.sin(phase))

def class_lookup(table, classes):
    picks = jnp.arange(table.shape[0], dtype=jnp.int32).reshape((-1,) + (1,) * classes.ndim)
    return lax.optimization_barrier(jnp.sum(jnp.where(classes[None] == picks, table.reshape(picks.shape), 0.0), axis=0))

def van_genuchten(pressure, alpha, power, conduct):
    suction = jnp.power(alpha * jnp.maximum(-pressure, 0.0), power)
    expo = 1.0 - 1.0 / power
    saturation = jnp.power(1.0 + suction, -expo)
    ratio = suction / (1.0 + suction)
    flow = conduct * jnp.sqrt(saturation) * jnp.square(1.0 - jnp.power(ratio, expo))
    return (saturation, flow)

def water_balance(padded, flow_pad, sat_new, sat_old, pores, conduct, codes, rows_glob, layers_glob, total_y, total_z):
    center = padded[1:-1, 1:-1]
    flow = flow_pad[1:-1, 1:-1]
    along = 0.5 * (flow[:, :, 1:] + flow[:, :, :-1]) * (center[:, :, 1:] - center[:, :, :-1])
    inflow = jnp.pad(along, ((0, 0), (0, 0), (0, 1))) - jnp.pad(along, ((0, 0), (0, 0), (1, 0)))
    upper_y = (rows_glob + 1 < total_y).astype(jnp.float32)[:, None, None]
    lower_y = (rows_glob > 0).astype(jnp.float32)[:, None, None]
    upper_z = (layers_glob + 1 < total_z).astype(jnp.float32)[None, :, None]
    lower_z = (layers_glob > 0).astype(jnp.float32)[None, :, None]
    inflow = inflow + upper_y * 0.5 * (flow + flow_pad[2:, 1:-1]) * (padded[2:, 1:-1] - center)
    inflow = inflow + lower_y * 0.5 * (flow + flow_pad[:-2, 1:-1]) * (padded[:-2, 1:-1] - center)
    inflow = inflow + upper_z * 0.5 * (flow + flow_pad[1:-1, 2:]) * (padded[1:-1, 2:] - center + 1.0)
    inflow = inflow + lower_z * 0.5 * (flow + flow_pad[1:-1, :-2]) * (padded[1:-1, :-2] - center - 1.0)
    surface_top = (layers_glob == total_z - 1).astype(jnp.float32)[None, :, None]
    bottom = (layers_glob == 0).astype(jnp.float32)[None, :, None]
    rainy = (codes == 1).astype(jnp.float32)[:, None, :]
    ponded = (codes == 2).astype(jnp.float32)[:, None, :]
    surface = rainy * RAINFALL + ponded * 2.0 * conduct * (0.5 - center)
    inflow = inflow + surface_top * surface - bottom * flow
    return STORAGE * pores * (sat_new - sat_old) - inflow

def reference(pressure_old, soil_class, top_code, retention_scale, retention_power, conductivity_sat, porosity, lift_weight, spectral_weight, local_weight, local_bias, project_weight, project_bias, output_weight):
    highest = lax.Precision.HIGHEST
    table_x = fourier_table(NX, 0, NX, M).astype(jnp.bfloat16).astype(jnp.float32)
    table_y = fourier_table(NY, 0, NY, M)
    table_z = fourier_table(NZ, 0, NZ, M)
    y_block = 4
    blocks = NY // y_block
    spans = 2 * M

    def lifted_rows(row_start):
        old_rows = lax.dynamic_slice_in_dim(pressure_old, row_start, y_block, 0)
        soil_rows = lax.dynamic_slice_in_dim(soil_class, row_start, y_block, 0)
        cell_k = class_lookup(conductivity_sat, soil_rows)
        lifted = (lift_weight[0][:, None, None, None] * (old_rows + 2.0)[None] + lift_weight[1][:, None, None, None] * jnp.log(cell_k)[None]).astype(jnp.bfloat16)
        lifted = lax.optimization_barrier(lifted)
        return (lifted.astype(jnp.float32), old_rows)

    def forward(total, block_index):
        row_start = block_index * y_block
        lifted, _ = lifted_rows(row_start)
        along_x = jnp.einsum('cyzx,ax->acyz', lifted, table_x)
        rows_y = lax.dynamic_slice_in_dim(table_y, row_start, y_block, 1)
        along_y = jnp.einsum('acyz,by->acbz', along_x, rows_y, precision=highest)
        return (total + jnp.einsum('acbz,dz->acbd', along_y, table_z, precision=highest), None)
    spectrum, _ = lax.scan(forward, jnp.zeros((spans, C, spans, spans), jnp.float32), jnp.arange(blocks, dtype=jnp.int32))
    spectrum = spectrum * (1.0 / math.sqrt(NX * NY * NZ))
    weights = spectral_weight.astype(jnp.float32).reshape(spans, spans, C, spans, C)
    mixed = jnp.einsum('acbd,abcdo->aobd', spectrum, weights, precision=highest)
    expanded = jnp.einsum('aobd,dz->aobz', mixed, table_z, precision=highest)
    scale_out = 1.0 / math.sqrt(spans ** 3)

    def tail(block_index):
        row_start = block_index * y_block
        lifted, old_rows = lifted_rows(row_start)
        rows_y = lax.dynamic_slice_in_dim(table_y, row_start, y_block, 1)
        modal = (jnp.einsum('aobz,by->aoyz', expanded, rows_y, precision=highest) * scale_out).astype(jnp.bfloat16)
        modal = lax.optimization_barrier(modal).astype(jnp.float32)
        spectral = jnp.einsum('aoyz,ax->oyzx', modal, table_x)
        local = jnp.einsum('co,cyzx->oyzx', local_weight.astype(jnp.float32), lifted)
        activated = jax.nn.gelu(spectral + local + local_bias[:, None, None, None]).astype(jnp.bfloat16)
        activated = lax.optimization_barrier(activated).astype(jnp.float32)
        hidden = jax.nn.gelu(jnp.einsum('cq,cyzx->qyzx', project_weight.astype(jnp.float32), activated) + project_bias[:, None, None, None]).astype(jnp.bfloat16)
        hidden = lax.optimization_barrier(hidden).astype(jnp.float32)
        return old_rows + jnp.einsum('q,qyzx->yzx', output_weight.astype(jnp.float32), hidden)
    pressure_new = lax.map(tail, jnp.arange(blocks, dtype=jnp.int32)).reshape(NY, NZ, NX)
    pressure_pad = jnp.pad(pressure_new, ((1, 1), (1, 1), (0, 0)))
    soil_pad = jnp.pad(soil_class, ((1, 1), (1, 1), (0, 0)))

    def residual_rows(block_index):
        row_start = block_index * y_block
        padded = lax.dynamic_slice_in_dim(pressure_pad, row_start, y_block + 2, 0)
        soil_rim = lax.dynamic_slice_in_dim(soil_pad, row_start, y_block + 2, 0)
        sat_pad, flow_pad = van_genuchten(padded, class_lookup(retention_scale, soil_rim), class_lookup(retention_power, soil_rim), class_lookup(conductivity_sat, soil_rim))
        soil_rows = lax.dynamic_slice_in_dim(soil_class, row_start, y_block, 0)
        old_rows = lax.dynamic_slice_in_dim(pressure_old, row_start, y_block, 0)
        cell_k = class_lookup(conductivity_sat, soil_rows)
        sat_old, _ = van_genuchten(old_rows, class_lookup(retention_scale, soil_rows), class_lookup(retention_power, soil_rows), cell_k)
        pores = class_lookup(porosity, soil_rows)
        codes = lax.dynamic_slice_in_dim(top_code, row_start, y_block, 0)
        rows_glob = row_start + jnp.arange(y_block, dtype=jnp.int32)
        layers_glob = jnp.arange(NZ, dtype=jnp.int32)
        return water_balance(padded, flow_pad, sat_pad[1:-1, 1:-1], sat_old, pores, cell_k, codes, rows_glob, layers_glob, NY, NZ)
    residual = lax.map(residual_rows, jnp.arange(blocks, dtype=jnp.int32)).reshape(NY, NZ, NX)
    return (pressure_new, residual)
```

```python
import math

import jax
import jax.numpy as jnp
import numpy as np
from jax import lax
from jax.experimental import pallas as pl
from jax.experimental.pallas import tpu as pltpu
from jax.sharding import PartitionSpec as P

M = 16
SPANS = 2 * M
C = 32
Q = 128
NX = 512
NY = 256
NZ = 256
DY = 16
DZ = 8
RY = NY // DY
RZ = NZ // DZ
RAINFALL = 0.5
STORAGE = 20.0
ROOT = math.sqrt(2.0 / math.pi)
CUBE = (0.044715 * ROOT) ** (1.0 / 3.0)
LINEAR = ROOT / CUBE
SCALE_IN = 1.0 / math.sqrt(NX * NY * NZ)
SCALE_OUT = 1.0 / math.sqrt(SPANS**3)
F32 = jnp.float32
BF16 = jnp.bfloat16
ACT = jnp.float32


def fourier_table(length):
    rows = np.arange(SPANS)
    freq = np.where(rows < M, rows + 1, rows - M + 1)
    phase = np.mod(freq[:, None] * np.arange(length)[None, :], length) * (2.0 * math.pi / length)
    return np.where((rows < M)[:, None], np.cos(phase), np.sin(phase)).astype(np.float32)


def as_bf16(table):
    return table.astype(jnp.bfloat16)


TABLE_X = as_bf16(fourier_table(NX))
TABLE_Y = fourier_table(NY)
TABLE_Z = fourier_table(NZ)


def split_table(table):
    high = as_bf16(table)
    low = as_bf16(table - high.astype(np.float32))
    return high, low


def split(value):
    high = value.astype(BF16)
    return high, (value - high.astype(F32)).astype(BF16)


def dot_nt(left, right):
    return lax.dot_general(left, right, (((1,), (1,)), ((), ())), preferred_element_type=F32)


def dot(left, right):
    return jnp.dot(left, right, preferred_element_type=F32)


def lookup(table_row, classes):
    rows, cols = classes.shape
    table = jnp.broadcast_to(table_row, (rows, 128))
    return jnp.concatenate(
        [
            jnp.take_along_axis(table, classes[:, i : i + 128], axis=1, mode="promise_in_bounds")
            for i in range(0, cols, 128)
        ],
        axis=1,
    )


def forward_kernel(p_ref, soil_ref, tab_ref, fxp_ref, out_ref):
    fxp = fxp_ref[...]
    for step in range(RY // 4):
        parts = []
        for t in range(4):
            y = 4 * step + t
            parts.append(p_ref[y] + 2.0)
            parts.append(lookup(tab_ref[5:6, :], soil_ref[y]))
        high, low = split(jnp.concatenate(parts, axis=0))
        out = dot_nt(fxp, high) + dot_nt(fxp, low)
        for t in range(4):
            piece = out[:, 64 * t : 64 * t + 64]
            out_ref[pl.ds(4 * step + t, DY, stride=RY), :] = jnp.concatenate(
                [piece[:DY], piece[DY:]], axis=1
            )


def gelu_scaled(v):
    u = v * (v * v + jnp.asarray(LINEAR, v.dtype))
    return v + v * jnp.tanh(u)


def saturation(head, log_alpha, power, expo):
    level = power * (log_alpha + jnp.log(jnp.maximum(-head, 1e-20)))
    root = jnp.exp(-0.5 * expo * jnp.log(1.0 + jnp.exp(level)))
    return level, root


def tail_kernel(
    e_ref,
    p_ref,
    soil_ref,
    top_ref,
    tab_ref,
    c2_ref,
    w2_ref,
    ow_ref,
    fzt_ref,
    fxb_ref,
    new_ref,
    res_ref,
    ey_ref,
    ez_ref,
    g_ref,
    prev_ref,
):
    y = pl.program_id(0)
    gz = lax.axis_index("gz")

    @pl.when(y == 0)
    def _():
        own = fzt_ref[pl.ds(pl.multiple_of(gz * RZ, RZ), RZ), :]
        rep = jnp.broadcast_to(own[:, None, :], (RZ, 8, 256)).reshape(256, 256)
        row = lax.broadcasted_iota(jnp.int32, (256, 256), 0)
        col = lax.broadcasted_iota(jnp.int32, (256, 256), 1)
        kron = jnp.where(lax.rem(row, 8) == lax.div(col, 32), rep, 0.0)
        k_hi, k_lo = split(kron)
        c2 = c2_ref[...]

        for yg in range(4):
            for oc in range(4):
                rows = jnp.concatenate(
                    [
                        jnp.concatenate(
                            [
                                e_ref[2 * oc + part, pl.ds(4 * yg + t, SPANS, stride=RY), :]
                                for part in range(2)
                            ],
                            axis=1,
                        )
                        for t in range(4)
                    ],
                    axis=0,
                )
                hi, lo = split(rows)
                g = dot_nt(k_hi, hi) + dot_nt(k_hi, lo) + dot_nt(k_lo, hi)
                g = (g * (SCALE_OUT * CUBE)).astype(BF16)
                for zg in range(4):
                    g_ref[yg, zg, 64 * oc : 64 * oc + 64, 0:128] = g[64 * zg : 64 * zg + 64]
            for zg in range(4):
                g_ref[yg, zg, :, 128:256] = c2

    yq = lax.div(y, 4)
    fx = fxb_ref[lax.rem(y, 4)]
    soil = soil_ref[0]
    old = p_ref[0]
    log_k = lookup(tab_ref[5:6, :], soil)
    base = old + 2.0
    zeros = jnp.zeros((64, NX), BF16)
    ones = jnp.ones((8, NX), F32)
    pad = (lax.broadcasted_iota(jnp.int32, (64, NX), 0) < 2).astype(F32).astype(BF16)
    news = []
    for zg in range(4):
        p8 = base[8 * zg : 8 * zg + 8]
        k8 = log_k[8 * zg : 8 * zg + 8]
        ph = p8.astype(BF16).astype(F32)
        kh = k8.astype(BF16).astype(F32)
        feat = jnp.concatenate([ph, p8 - ph, ph, kh, k8 - kh, kh, ones, ones], axis=0).astype(BF16)
        rhs = jnp.concatenate([fx, feat, zeros], axis=0)
        act = gelu_scaled(dot(g_ref[yq, zg], rhs).astype(ACT)).astype(BF16)
        total = None
        for zp in range(4):
            chunk = jnp.concatenate(
                [act[64 * oc + 16 * zp : 64 * oc + 16 * zp + 16] for oc in range(4)] + [pad], axis=0
            )
            hid = gelu_scaled(dot(w2_ref[...], chunk).astype(ACT)).astype(BF16)
            part = dot(ow_ref[:, 256 * zp : 256 * zp + 256], hid)
            total = part if total is None else total + part
        news.append(old[8 * zg : 8 * zg + 8] + total[:8] * (0.5 / CUBE))
    head = jnp.concatenate(news, axis=0)
    new_ref[0] = head

    log_alpha = lookup(tab_ref[0:1, :], soil)
    power = lookup(tab_ref[1:2, :], soil)
    expo = lookup(tab_ref[2:3, :], soil)
    conduct = lookup(tab_ref[3:4, :], soil)
    pores = lookup(tab_ref[4:5, :], soil)
    _, root_old = saturation(old, log_alpha, power, expo)
    level, root = saturation(head, log_alpha, power, expo)
    ratio = jnp.exp(-expo * jnp.log(1.0 + jnp.exp(-level)))
    flow = conduct * root * jnp.square(1.0 - ratio)
    store = pores * (root * root - root_old * root_old)

    lane = lax.broadcasted_iota(jnp.int32, (RZ, NX), 1)
    row = lax.broadcasted_iota(jnp.int32, (RZ, NX), 0)
    along = 0.5 * (flow + pltpu.roll(flow, NX - 1, 1)) * (pltpu.roll(head, NX - 1, 1) - head)
    along = jnp.where(lane == NX - 1, 0.0, along)
    inflow = along - pltpu.roll(along, 1, 1)
    down = 0.5 * (flow + pltpu.roll(flow, RZ - 1, 0)) * (pltpu.roll(head, RZ - 1, 0) - head + 1.0)
    down = jnp.where(row == RZ - 1, 0.0, down)
    inflow = inflow + down - pltpu.roll(down, 1, 0)
    code = jnp.broadcast_to(top_ref[pl.ds(y, 1), :], (RZ, NX))
    surface = jnp.where(code == 1, RAINFALL, 0.0) + jnp.where(
        code == 2, 2.0 * conduct * (0.5 - head), 0.0
    )
    top_row = jnp.where(gz == DZ - 1, RZ - 1, RZ)
    bottom_row = jnp.where(gz == 0, 0, RZ)
    inflow = inflow + jnp.where(row == top_row, surface, 0.0)
    inflow = inflow - jnp.where(row == bottom_row, flow, 0.0)
    value = store - inflow

    @pl.when(y == 0)
    def _():
        res_ref[0] = value
        ey_ref[0, 0] = head
        ey_ref[0, 1] = flow

    @pl.when(y > 0)
    def _():
        cross = 0.5 * (flow + prev_ref[1]) * (head - prev_ref[0])
        res_ref[y - 1] = res_ref[y - 1] - cross
        res_ref[y] = value + cross

    @pl.when(y == RY - 1)
    def _():
        ey_ref[1, 0] = head
        ey_ref[1, 1] = flow

    prev_ref[0] = head
    prev_ref[1] = flow
    ez_ref[0, 0, pl.ds(y, 1), :] = head[0:1]
    ez_ref[0, 1, pl.ds(y, 1), :] = flow[0:1]
    ez_ref[1, 0, pl.ds(y, 1), :] = head[RZ - 1 : RZ]
    ez_ref[1, 1, pl.ds(y, 1), :] = flow[RZ - 1 : RZ]


def rim_kernel(res_ref, ey_ref, ez_ref, before_y, after_y, before_z, after_z, out_ref):
    gy = lax.axis_index("gy")
    gz = lax.axis_index("gz")
    out_ref[...] = res_ref[...]

    def gain(own, edge, other, shift):
        return 0.5 * (own[edge, 1] + other[1]) * (other[0] - own[edge, 0] + shift)

    @pl.when(gy > 0)
    def _():
        out_ref[0] = out_ref[0] - gain(ey_ref, 0, before_y, 0.0)

    @pl.when(gy < DY - 1)
    def _():
        out_ref[RY - 1] = out_ref[RY - 1] - gain(ey_ref, 1, after_y, 0.0)

    @pl.when(gz > 0)
    def _():
        add = gain(ez_ref, 0, before_z, -1.0)
        for y in range(RY):
            out_ref[y, 0:1, :] = out_ref[y, 0:1, :] - add[y : y + 1]

    @pl.when(gz < DZ - 1)
    def _():
        add = gain(ez_ref, 1, after_z, 1.0)
        for y in range(RY):
            out_ref[y, RZ - 1 : RZ, :] = out_ref[y, RZ - 1 : RZ, :] - add[y : y + 1]


def full(shape):
    return pl.BlockSpec(shape, lambda *_: (0,) * len(shape))


def split_xla(value):
    high = lax.reduce_precision(value, 8, 7)
    return high, lax.reduce_precision(value - high, 8, 7)


def constants():
    fxp = TABLE_X.reshape(DY, 2, NX).transpose(1, 0, 2).reshape(SPANS, NX)
    fxb = np.zeros((4, 4, SPANS, NX), dtype=TABLE_X.dtype)
    for t in range(4):
        fxb[t, t] = TABLE_X
    fzt = np.tile(TABLE_Z.T, (1, 8))
    return fxp, fxb.reshape(4, 128, NX), fzt


def expand_table():
    table = TABLE_Y.reshape(DZ, 4, DY, RY)
    out = np.zeros((DY, 2, RY, DZ, 2, 4), np.float32)
    for a in range(2):
        out[:, a, :, :, a, :] = table.transpose(2, 3, 0, 1)
    return out.reshape(DY * 2 * RY, DZ * 8)


def shards(
    pressure_old,
    soil_class,
    top_code,
    retention_scale,
    retention_power,
    conductivity_sat,
    porosity,
    lift_weight,
    spectral_weight,
    local_weight,
    local_bias,
    project_weight,
    project_bias,
    output_weight,
):
    highest = lax.Precision.HIGHEST
    fxp, fxb, fzt = constants()
    rows = jnp.stack(
        [
            jnp.log(retention_scale),
            retention_power,
            1.0 - 1.0 / retention_power,
            conductivity_sat,
            STORAGE * porosity,
            jnp.log(conductivity_sat),
            jnp.zeros_like(porosity),
            jnp.zeros_like(porosity),
        ]
    )
    tab = jnp.pad(rows, ((0, 0), (0, 128 - rows.shape[1])))
    sent = pl.pallas_call(
        forward_kernel,
        out_shape=jax.ShapeDtypeStruct((DY * RY, 128), F32),
        name="forward",
    )(pressure_old, soil_class, tab, fxp)
    moved = lax.all_to_all(sent.reshape(DY, RY, 128), "gy", 0, 0, tiled=True)
    along_y = jnp.dot(TABLE_Y, moved.reshape(NY, 128), precision=highest)
    gz = lax.axis_index("gz")
    own_z = lax.dynamic_slice_in_dim(jnp.asarray(TABLE_Z), gz * RZ, RZ, 1)
    part = jnp.einsum("bkz,dz->bkd", along_y.reshape(SPANS, 4, RZ), own_z, precision=highest)
    pieces = lax.all_to_all(part.reshape(DZ, 4, 4, SPANS), "gz", 0, 0, tiled=True)
    spectrum = jnp.sum(pieces, axis=0).reshape(4, 2, 2, SPANS) * SCALE_IN
    weights = spectral_weight.astype(F32).reshape(2, 4, C, SPANS, C)
    folded = jnp.einsum("fc,abcdo->fabod", lift_weight, weights, precision=highest)
    mixed = jnp.sum(spectrum.transpose(2, 1, 0, 3)[:, :, :, None, :] * folded, axis=0)
    gathered = lax.all_gather(mixed.reshape(8, C * SPANS), "gz", axis=0)
    spread = jnp.einsum(
        "irk,ktl->itrl",
        expand_table().reshape(DY, 2 * RY, DZ * 8),
        gathered.reshape(DZ * 8, 8, 128),
        precision=highest,
    )
    modal = lax.all_to_all(spread, "gy", 0, 0, tiled=True)
    modal = modal.transpose(1, 0, 2, 3).reshape(8, SPANS * RY, 128)

    coef = jnp.dot(lift_weight, local_weight.astype(F32), precision=highest) * CUBE
    c_hi, c_lo = split_xla(coef)
    b_hi, b_lo = split_xla(local_bias * CUBE)
    kinds = jnp.stack([c_hi[0], c_hi[0], c_lo[0], c_hi[1], c_hi[1], c_lo[1], b_hi, b_lo])
    eye8 = np.eye(8, dtype=np.float32)
    c2 = jnp.einsum("tuv,zw->uzvtw", kinds.reshape(8, 4, 8), eye8, precision=highest)
    c2 = jnp.pad(c2.reshape(256, 64), ((0, 0), (0, 64))).astype(BF16)
    eye2 = np.eye(2, dtype=np.float32)
    half = (project_weight.astype(F32) * 0.5).reshape(4, 8, Q)
    w2 = jnp.einsum("uvq,zw->zquwv", half, eye2, precision=highest).reshape(256, 64)
    p_hi, p_lo = split_xla(project_bias * CUBE)
    tail_cols = jnp.tile(jnp.stack([p_hi, p_lo], axis=1), (2, 1))
    w2 = jnp.concatenate([w2, tail_cols, jnp.zeros((256, 62), F32)], axis=1).astype(BF16)
    ow = (np.eye(16, 8, dtype=np.float32)[:, :, None] * output_weight.astype(F32)).reshape(16, 1024)
    ow = ow.astype(BF16)

    row_block = pl.BlockSpec((1, RZ, NX), lambda y: (y, 0, 0))
    pressure_new, partial_res, edge_y, edge_z = pl.pallas_call(
        tail_kernel,
        grid=(RY,),
        in_specs=[
            full((8, SPANS * RY, 128)),
            row_block,
            row_block,
            full((RY, NX)),
            full((8, 128)),
            full((256, 128)),
            full((256, 128)),
            full((16, 1024)),
            full((NZ, 256)),
            full((4, 128, NX)),
        ],
        out_specs=[row_block, full((RY, RZ, NX)), full((2, 2, RZ, NX)), full((2, 2, RY, NX))],
        out_shape=[
            jax.ShapeDtypeStruct((RY, RZ, NX), F32),
            jax.ShapeDtypeStruct((RY, RZ, NX), F32),
            jax.ShapeDtypeStruct((2, 2, RZ, NX), F32),
            jax.ShapeDtypeStruct((2, 2, RY, NX), F32),
        ],
        scratch_shapes=[pltpu.VMEM((4, 4, 256, 256), BF16), pltpu.VMEM((2, RZ, NX), F32)],
        name="tail",
    )(modal, pressure_old, soil_class, top_code, tab, c2, w2, ow, fzt, fxb)

    up_y = [(i, i + 1) for i in range(DY - 1)]
    up_z = [(i, i + 1) for i in range(DZ - 1)]
    before_y = lax.ppermute(edge_y[1], "gy", up_y)
    after_y = lax.ppermute(edge_y[0], "gy", [(j, i) for i, j in up_y])
    before_z = lax.ppermute(edge_z[1], "gz", up_z)
    after_z = lax.ppermute(edge_z[0], "gz", [(j, i) for i, j in up_z])
    residual = pl.pallas_call(
        rim_kernel,
        out_shape=jax.ShapeDtypeStruct((RY, RZ, NX), F32),
        name="rim",
    )(partial_res, edge_y, edge_z, before_y, after_y, before_z, after_z)
    return (pressure_new, residual)


def solution(mesh):
    return jax.shard_map(
        shards,
        mesh=mesh,
        in_specs=(
            P("gy", "gz", None),
            P("gy", "gz", None),
            P("gy", None),
            P(),
            P(),
            P(),
            P(),
            P(),
            P("gy", "gz", None, None),
            P(),
            P(),
            P(),
            P(),
            P(),
        ),
        out_specs=(P("gy", "gz", None), P("gy", "gz", None)),
        check_vma=False,
    )
```
